32 devices in a mesh: sect: 4 (over y, x), dev: 8 (over z, core).
Axes of the slice: x: 2, y: 2, z: 4, core: 2. Of those that a mesh axis runs over, the one named last changes fastest.
Arguments:
- voltages: bfloat16 [2, 2048, 65536], P(None, 'sect', 'dev'), may hold values from -6 to 6
- filter_taps: float32 [4, 1024], replicated, may hold values from -3 to 3
- feed_tile: int32 [2048], P('sect'), may hold values from 0 to 127
- bad_feed: int32 [2048], P('sect'), may hold values 0 or 1
- delays: float32 [1024, 128], P('sect'), may hold values from -32 to 32
Outputs:
- visibilities: float32 [2, 1024, 128, 128], P(None, 'dev', 'sect')
- beams: bfloat16 [2, 1024, 1024, 64], P(None, 'dev', 'sect')
The draws below stay inside these ranges and needn't reach their ends.
Inputs may be any that keep to these rules, and one draw needn't show every extreme that they name: `feed_tile`: each feed belongs to one tile.
All inputs are finite; a program needn't handle non-finite values. No bound on the sum of `bad_feed` on one device may be relied on, other than what follows from the above.
Results may differ from the reference program's by a relative error of at most 0.014.
Values may be sent and summed in bfloat16 or wider, within the bound.
A program may use at most 192 MiB of HBM per device.

```python
import math
import jax
import jax.numpy as jnp
from jax import lax

FEEDS = 2048
CHANNELS = 1024
TILES = 128
BEAMS = 1024
TAPS = 4
FRAMES = 64
SAMPLES = 65536
N_SECT = 4


def place_ends(entries, rng, low, top_value):
    extent = entries.shape
    index_at = [jax.random.randint(jax.random.fold_in(rng, axis), (), 0, extent[axis]) for axis in range(len(extent))]
    entries = entries.at[tuple(index_at)].set(low)
    longest = extent.index(max(extent))
    index_at[longest] = (index_at[longest] + 1) % extent[longest]
    return entries.at[tuple(index_at)].set(top_value)


def steps_of(key, dims, shards, low, largest):
    factor_of = 1.0
    for dim, parts in shards:
        draws = jax.random.uniform(jax.random.fold_in(jax.random.fold_in(key, 6), dim), (parts,), jnp.float32, low / len(shards), largest / len(shards))
        factor_of = factor_of * jnp.repeat(jnp.exp(draws), dims[dim] // parts).reshape((-1,) + (1,) * (len(dims) - 1 - dim))
    return factor_of


def bell_draw(key, dims, scale, bound, shards=(), kind=jnp.bfloat16):
    gain = steps_of(key, dims, shards, -0.22, 0.18) if shards else 1.0
    drawn = jax.random.normal(key, dims, jnp.float32) * scale * gain
    return jnp.minimum(jnp.maximum(drawn, -bound), bound).astype(kind)


def setup_inputs(seed: int = 0) -> dict:
    key_list = jax.random.split(jax.random.key(seed), 6)
    voltages = bell_draw(key_list[0], (2, FEEDS, SAMPLES), 1.0, 6.0, ((1, 4), (2, 8)))
    filter_taps = bell_draw(key_list[1], (TAPS, CHANNELS), 0.5, 3.0, (), jnp.float32)
    feed_tile = place_ends(jax.random.randint(key_list[2], (FEEDS,), 0, TILES), jax.random.fold_in(key_list[2], 1), 0, TILES - 1).astype(jnp.int32)
    bad_feed = place_ends((jax.random.randint(key_list[3], (FEEDS,), 0, 8) < 1).astype(jnp.int32), jax.random.fold_in(key_list[3], 1), 0, 1)
    delays = jnp.clip(jax.random.uniform(key_list[4], (BEAMS, TILES), jnp.float32, -32.0, 32.0) * steps_of(key_list[4], (BEAMS, TILES), ((0, 4),), -0.4, 0.0), -32.0, 32.0)
    return {"voltages": voltages, "filter_taps": filter_taps, "feed_tile": feed_tile, "bad_feed": bad_feed, "delays": delays}


def fourier_tables():
    positions = jnp.arange(CHANNELS, dtype=jnp.int32)
    product = positions[:, None] * positions[None, :] % CHANNELS
    phase_angle = product.astype(jnp.float32) * (2.0 * math.pi / CHANNELS)
    factor = 1.0 / math.sqrt(CHANNELS)
    cosine_table = (jnp.cos(phase_angle) * factor).astype(jnp.bfloat16)
    sine_table = (jnp.sin(phase_angle) * factor).astype(jnp.bfloat16)
    return (cosine_table, sine_table)

def filter_bank(window, filter_taps, frames):
    running = jnp.zeros((2, window.shape[1], frames, window.shape[3]), jnp.float32)
    for tap_index in range(TAPS):
        begin_frame = TAPS - 1 - tap_index
        running = running + filter_taps[tap_index] * window[:, :, begin_frame:begin_frame + frames].astype(jnp.float32)
    return running.astype(jnp.bfloat16)

def transform(filtered, cosine_table, sine_table):
    real_part = jnp.dot(filtered[0], cosine_table, preferred_element_type=jnp.float32) + jnp.dot(filtered[1], sine_table, preferred_element_type=jnp.float32)
    quad_part = jnp.dot(filtered[1], cosine_table, preferred_element_type=jnp.float32) - jnp.dot(filtered[0], sine_table, preferred_element_type=jnp.float32)
    return jnp.stack([real_part, quad_part]).astype(jnp.bfloat16)

def tile_matrix(feed_tile, bad_feed):
    tile_ids = jnp.arange(TILES, dtype=jnp.int32)
    member = (feed_tile[:, None] == tile_ids[None, :]) & (bad_feed[:, None] == 0)
    return jnp.where(member, 1.0, 0.0).astype(jnp.bfloat16)

def reference(voltages, filter_taps, feed_tile, bad_feed, delays):
    cosine_table, sine_table = fourier_tables()
    block_feeds = FEEDS // N_SECT

    def add_section(section, running):
        first_feed = (section * block_feeds).astype(jnp.int32)
        block = lax.dynamic_slice_in_dim(voltages, first_feed, block_feeds, 1)
        block = block.reshape(2, block_feeds, FRAMES, CHANNELS)
        window = jnp.pad(block, ((0, 0), (0, 0), (TAPS - 1, 0), (0, 0)))
        spectra = transform(filter_bank(window, filter_taps, FRAMES), cosine_table, sine_table)
        matrix = tile_matrix(lax.dynamic_slice_in_dim(feed_tile, first_feed, block_feeds, 0), lax.dynamic_slice_in_dim(bad_feed, first_feed, block_feeds, 0))
        partial_value = jnp.einsum('zfnc,fa->zanc', spectra.astype(jnp.float32), matrix.astype(jnp.float32))
        rounded = lax.optimization_barrier(partial_value.astype(jnp.bfloat16))
        return running + rounded.astype(jnp.float32)
    initial = jnp.zeros((2, TILES, FRAMES, CHANNELS), jnp.float32)
    running = lax.fori_loop(0, N_SECT, add_section, initial)
    tile_volts = running.astype(jnp.bfloat16)
    volts_real = tile_volts[0].astype(jnp.float32)
    volts_quad = tile_volts[1].astype(jnp.float32)
    vis_scale = 1.0 / (FRAMES * FEEDS / TILES)
    real_part = jnp.einsum('atc,btc->cab', volts_real, volts_real) + jnp.einsum('atc,btc->cab', volts_quad, volts_quad)
    quad_part = jnp.einsum('atc,btc->cab', volts_quad, volts_real) - jnp.einsum('atc,btc->cab', volts_real, volts_quad)
    visibilities = jnp.stack([real_part, quad_part]) * vis_scale
    channel = jnp.arange(CHANNELS, dtype=jnp.int32).astype(jnp.float32)
    block_beams = BEAMS // N_SECT

    def beam_block(section):
        delay_rows = lax.dynamic_slice_in_dim(delays, (section * block_beams).astype(jnp.int32), block_beams, 0)
        phase_angle = delay_rows[None, :, :] * channel[:, None, None] * (2.0 * math.pi / CHANNELS)
        weight_cos = jnp.cos(phase_angle).astype(jnp.bfloat16).astype(jnp.float32)
        weight_sin = jnp.sin(phase_angle).astype(jnp.bfloat16).astype(jnp.float32)
        beam_real = jnp.einsum('cba,atc->cbt', weight_cos, volts_real) + jnp.einsum('cba,atc->cbt', weight_sin, volts_quad)
        beam_quad = jnp.einsum('cba,atc->cbt', weight_cos, volts_quad) - jnp.einsum('cba,atc->cbt', weight_sin, volts_real)
        return jnp.stack([beam_real, beam_quad])
    stacked = lax.map(beam_block, jnp.arange(N_SECT, dtype=jnp.int32))
    beams = jnp.transpose(stacked, (1, 2, 0, 3, 4)).reshape(2, CHANNELS, BEAMS, FRAMES)
    beams = (beams * (1.0 / math.sqrt(FEEDS))).astype(jnp.bfloat16)
    return (visibilities, beams)
```

```python
import math

import jax
import jax.numpy as jnp
from jax import lax
from jax.sharding import PartitionSpec as P

FEEDS = 2048
TILES = 128
TAPS = 4


def shifted(x, axis, by):
    size = lax.axis_size(axis)
    pairs = [(i, i + by) for i in range(size) if 0 <= i + by < size]
    return lax.ppermute(x, axis, pairs)


def turn_trig(turns):
    r = turns - jnp.round(turns)
    y = r * math.pi
    q = y * y
    s = 0.0
    for n in (11, 9, 7, 5, 3, 1):
        s = s * q + (-1.0) ** ((n - 1) // 2) / math.factorial(n)
    s = s * y
    c = 0.0
    for n in (12, 10, 8, 6, 4, 2, 0):
        c = c * q + (-1.0) ** (n // 2) / math.factorial(n)
    return 1.0 - 2.0 * s * s, 2.0 * s * c


def fourier_tables(channels):
    low = 32
    c = jnp.arange(channels, dtype=jnp.int32)[None, :]
    k_high = low * jnp.arange(channels // low, dtype=jnp.int32)[:, None]
    k_low = jnp.arange(low, dtype=jnp.int32)[:, None]
    ca, sa = turn_trig((k_high * c % channels).astype(jnp.float32) / channels)
    cb, sb = turn_trig((k_low * c % channels).astype(jnp.float32) / channels)
    factor = 1.0 / math.sqrt(channels)
    ca, sa = (ca * factor)[:, None], (sa * factor)[:, None]
    cb, sb = cb[None], sb[None]
    cosine = (ca * cb - sa * sb).astype(jnp.bfloat16).reshape(channels, channels)
    sine = (sa * cb + ca * sb).astype(jnp.bfloat16).reshape(channels, channels)
    return cosine, sine


def beam_weights(delays, first, count, channels):
    low = 16
    d = delays.T[None]
    high = (first + low * jnp.arange(count // low, dtype=jnp.int32)).astype(jnp.float32)
    ca, sa = turn_trig(d * high[:, None, None] / channels)
    cb, sb = turn_trig(d * jnp.arange(low, dtype=jnp.float32)[:, None, None] / channels)
    ca, sa, cb, sb = ca[:, None], sa[:, None], cb[None], sb[None]
    shape = (count,) + d.shape[1:]
    cosine = (ca * cb - sa * sb).astype(jnp.bfloat16).reshape(shape)
    sine = (sa * cb + ca * sb).astype(jnp.bfloat16).reshape(shape)
    return jnp.concatenate([cosine, sine], axis=1)


def local(voltages, filter_taps, feed_tile, bad_feed, delays):
    channels = filter_taps.shape[1]
    local_frames = voltages.shape[2] // channels
    rim = (TAPS - 1) * channels
    n_dev = lax.axis_size("dev")
    local_chans = channels // n_dev
    total_frames = local_frames * n_dev

    tile_ids = jnp.arange(TILES, dtype=jnp.int32)
    member = (feed_tile[None, :] == tile_ids[:, None]) & (bad_feed[None, :] == 0)
    matrix = jnp.where(member, 1.0, 0.0).astype(jnp.bfloat16)
    partial_value = jnp.einsum(
        "af,zfs->zas", matrix, voltages, preferred_element_type=jnp.float32
    ).astype(jnp.bfloat16)
    summed = lax.psum_scatter(partial_value, "sect", scatter_dimension=1, tiled=True)
    own = summed.shape[1]

    history = shifted(summed[:, :, summed.shape[2] - rim :], "dev", 1)
    window = jnp.concatenate([history, summed], axis=2).reshape(
        2, own, local_frames + TAPS - 1, channels
    )
    running = 0.0
    for tap in range(TAPS):
        begin = TAPS - 1 - tap
        running = running + filter_taps[tap] * window[:, :, begin : begin + local_frames].astype(
            jnp.float32
        )
    filtered = running.astype(jnp.bfloat16)

    cosine, sine = fourier_tables(channels)
    dot = lambda a, b: jnp.dot(a, b, preferred_element_type=jnp.float32)
    spectra = jnp.stack(
        [
            dot(filtered[0], cosine) + dot(filtered[1], sine),
            dot(filtered[1], cosine) - dot(filtered[0], sine),
        ]
    ).astype(jnp.bfloat16)

    own_tiles = lax.all_to_all(spectra, "dev", split_axis=3, concat_axis=2, tiled=True)
    gathered = lax.all_gather(own_tiles, "sect", axis=1, tiled=True)

    volts = jnp.transpose(gathered, (3, 0, 2, 1))
    mine = jnp.transpose(own_tiles, (3, 0, 1, 2))
    left_real = jnp.concatenate([mine[:, 0], mine[:, 1]], axis=2)
    left_quad = jnp.concatenate([mine[:, 1], -mine[:, 0]], axis=2)
    left = jnp.concatenate([left_real, left_quad], axis=1)
    right = volts.reshape(local_chans, 2 * total_frames, TILES)
    vis = jnp.einsum("cat,ctb->cab", left, right, preferred_element_type=jnp.float32)
    vis_scale = 1.0 / (total_frames * FEEDS / TILES)
    vis = vis * vis_scale
    visibility = jnp.stack([vis[:, :own], vis[:, own:]])

    weights = beam_weights(
        delays, lax.axis_index("dev") * local_chans, local_chans, channels
    )
    rows = jnp.concatenate(
        [
            jnp.concatenate([volts[:, 0], volts[:, 1]], axis=2),
            jnp.concatenate([volts[:, 1], -volts[:, 0]], axis=2),
        ],
        axis=1,
    )
    beams = jnp.einsum("cna,cab->cnb", rows, weights, preferred_element_type=jnp.float32)
    beams = (beams * (1.0 / math.sqrt(FEEDS))).astype(jnp.bfloat16)
    beams = beams.reshape(local_chans, 2, total_frames, weights.shape[2])
    return visibility, jnp.transpose(beams, (1, 0, 3, 2))


def solution(mesh):
    return jax.shard_map(
        local,
        mesh=mesh,
        in_specs=(P(None, "sect", "dev"), P(), P("sect"), P("sect"), P("sect", None)),
        out_specs=(P(None, "dev", "sect", None), P(None, "dev", "sect", None)),
        check_vma=False,
    )
```

```python
import functools
import math

import jax
import jax.numpy as jnp
from jax import lax
from jax.experimental import pallas as pl
from jax.experimental.pallas import tpu as pltpu
from jax.sharding import PartitionSpec as P

FEEDS = 2048
TILES = 128
TAPS = 4


def shifted(x, axis, by):
    size = lax.axis_size(axis)
    pairs = [(i, i + by) for i in range(size) if 0 <= i + by < size]
    return lax.ppermute(x, axis, pairs)


def turn_trig(turns):
    r = turns - jnp.round(turns)
    y = r * math.pi
    q = y * y
    s = 0.0
    for n in (11, 9, 7, 5, 3, 1):
        s = s * q + (-1.0) ** ((n - 1) // 2) / math.factorial(n)
    s = s * y
    c = 0.0
    for n in (12, 10, 8, 6, 4, 2, 0):
        c = c * q + (-1.0) ** (n // 2) / math.factorial(n)
    return 1.0 - 2.0 * s * s, 2.0 * s * c


def fourier_tables(channels):
    low = 32
    c = jnp.arange(channels, dtype=jnp.int32)[None, :]
    k_high = low * jnp.arange(channels // low, dtype=jnp.int32)[:, None]
    k_low = jnp.arange(low, dtype=jnp.int32)[:, None]
    ca, sa = turn_trig((k_high * c % channels).astype(jnp.float32) / channels)
    cb, sb = turn_trig((k_low * c % channels).astype(jnp.float32) / channels)
    factor = 1.0 / math.sqrt(channels)
    ca, sa = (ca * factor)[:, None], (sa * factor)[:, None]
    cb, sb = cb[None], sb[None]
    cosine = (ca * cb - sa * sb).astype(jnp.bfloat16).reshape(channels, channels)
    sine = (sa * cb + ca * sb).astype(jnp.bfloat16).reshape(channels, channels)
    return cosine, sine


def beam_weights(delays, first, count, channels):
    low = 16
    d = delays.T[None]
    high = (first + low * jnp.arange(count // low, dtype=jnp.int32)).astype(jnp.float32)
    ca, sa = turn_trig(d * high[:, None, None] / channels)
    cb, sb = turn_trig(d * jnp.arange(low, dtype=jnp.float32)[:, None, None] / channels)
    ca, sa, cb, sb = ca[:, None], sa[:, None], cb[None], sb[None]
    shape = (count,) + d.shape[1:]
    cosine = (ca * cb - sa * sb).astype(jnp.bfloat16).reshape(shape)
    sine = (sa * cb + ca * sb).astype(jnp.bfloat16).reshape(shape)
    return jnp.concatenate([cosine, sine], axis=1)


VMEM = pl.BlockSpec(memory_space=pltpu.VMEM)


def transform_kernel(summed, history, taps, cosine, sine, out, filtered):
    n_dest, _, _, width = out.shape
    own = summed.shape[1]
    channels = taps.shape[1]
    frames = summed.shape[2] // channels
    for z in range(2):
        for t in range(frames):
            total = 0.0
            for m in range(TAPS):
                if t >= m:
                    block = summed[z, :, (t - m) * channels : (t - m + 1) * channels]
                else:
                    at = t - m + TAPS - 1
                    block = history[z, :, at * channels : (at + 1) * channels]
                total = total + taps[m : m + 1, :] * block.astype(jnp.float32)
            filtered[z, t * own : (t + 1) * own, :] = total.astype(jnp.bfloat16)
    step = max(256, width)
    dot = lambda a, b: jnp.dot(a, b, preferred_element_type=jnp.float32)
    for begin in range(0, channels, step):
        c, s = cosine[:, begin : begin + step], sine[:, begin : begin + step]
        real = (dot(filtered[0], c) + dot(filtered[1], s)).astype(jnp.bfloat16)
        quad = (dot(filtered[1], c) - dot(filtered[0], s)).astype(jnp.bfloat16)
        for j in range(step // width):
            out[begin // width + j, 0] = real[:, j * width : (j + 1) * width]
            out[begin // width + j, 1] = quad[:, j * width : (j + 1) * width]


def exchange_kernel(n_sect, n_dev, src, out, own_sem, a_send, a_recv, x_send, x_recv, y_send, y_recv):
    me_s, me_d = lax.axis_index("sect"), lax.axis_index("dev")
    rows = n_sect // 2
    side, row = lax.rem(me_s, 2), me_s // 2
    across = row * 2 + 1 - side
    others = [(lax.rem(row + j, rows) * 2 + side) for j in range(1, rows)]
    senders = [(lax.rem(row + rows - j, rows) * 2 + side) for j in range(1, rows)]

    barrier = pltpu.get_barrier_semaphore()
    mesh_id = pl.DeviceIdType.MESH
    for o in range(1, n_dev):
        pl.semaphore_signal(barrier, inc=1, device_id=(me_s, lax.rem(me_d + o, n_dev)), device_id_type=mesh_id)
    for s in [across] + others:
        pl.semaphore_signal(barrier, inc=1, device_id=(s, me_d), device_id_type=mesh_id)
    pl.semaphore_wait(barrier, n_dev - 1 + rows)

    def push(source, target, send, recv, device):
        return pltpu.make_async_remote_copy(
            src_ref=source, dst_ref=target, send_sem=send, recv_sem=recv,
            device_id=device, device_id_type=mesh_id,
        )

    order = [0] + [o for pair in zip(range(1, n_dev), range(n_dev - 1, 0, -1)) for o in pair][: n_dev - 1]
    keep = pltpu.make_async_copy(src.at[me_d], out.at[me_s, me_d], own_sem)
    keep.start()
    sends = []
    to_dev = {}
    for o in order[1:]:
        dest = lax.rem(me_d + o, n_dev)
        to_dev[o] = push(src.at[dest], out.at[me_s, me_d], a_send.at[o], a_recv.at[o], (me_s, dest))
        to_dev[o].start()
    keep.wait()

    first = {}

    def spread(o):
        p = lax.rem(me_d + n_dev - o, n_dev)
        here = out.at[me_s, p]
        if o:
            to_dev[o].wait_recv()
        first[o, 0] = push(here, here, x_send.at[o, 0], x_recv.at[o, 0], (across, me_d))
        first[o, 0].start()
        for j in range(1, rows):
            first[o, j] = push(here, here, y_send.at[o, j, 0], y_recv.at[o, j, 0], (others[j - 1], me_d))
            first[o, j].start()

    def relay(o, by_side):
        p = lax.rem(me_d + n_dev - o, n_dev)
        first[o, 0].wait_recv()
        for j in range(1, rows):
            first[o, j].wait_recv()
        for j in range(1, rows):
            if by_side:
                block = out.at[across, p]
                copy = push(block, block, y_send.at[o, j, 1], y_recv.at[o, j, 1], (others[j - 1], me_d))
            else:
                block = out.at[senders[j - 1], p]
                copy = push(block, block, x_send.at[o, j], x_recv.at[o, j], (across, me_d))
            copy.start()
            sends.append(copy)

    lag = 1
    for i in range(n_dev + lag):
        if i < n_dev:
            spread(order[i])
        if i >= lag:
            relay(order[i - lag], (i - lag) % 2 == 0)
    for copy in sends:
        copy.wait_recv()
    for copy in list(to_dev.values()) + list(first.values()) + sends:
        copy.wait_send()


def exchange(blocks, n_sect, n_dev):
    rows = n_sect // 2
    dma = pltpu.SemaphoreType.DMA
    return pl.pallas_call(
        functools.partial(exchange_kernel, n_sect, n_dev),
        out_shape=jax.ShapeDtypeStruct((n_sect,) + blocks.shape, blocks.dtype),
        in_specs=[VMEM],
        out_specs=VMEM,
        scratch_shapes=[
            dma, dma((n_dev,)), dma((n_dev,)),
            dma((n_dev, rows)), dma((n_dev, rows)),
            dma((n_dev, rows, 2)), dma((n_dev, rows, 2)),
        ],
        compiler_params=pltpu.CompilerParams(
            collective_id=0, has_side_effects=True, vmem_limit_bytes=32 * 2**20
        ),
    )(blocks)


def product_kernel(own, vis_scale, beam_scale, volts, weights, vis, beams, full):
    first = pl.multiple_of(lax.axis_index("sect") * own, own)
    count, both, _ = volts.shape
    half = both // 2

    @pl.loop(0, count)
    def _(c):
        real, quad = volts[c, :half, :], volts[c, half:, :]
        rows = jnp.concatenate(
            [jnp.concatenate([real, quad], axis=1), jnp.concatenate([quad, -real], axis=1)], axis=0
        )
        beam = jnp.dot(rows, weights[c], preferred_element_type=jnp.float32) * beam_scale
        beams[0, c] = beam[:half].astype(jnp.bfloat16)
        beams[1, c] = beam[half:].astype(jnp.bfloat16)
        right = jnp.concatenate([real, quad], axis=0)
        turned = jnp.concatenate([quad, -real], axis=0)
        over_time = (((0,), (0,)), ((), ()))
        full[0] = lax.dot_general(right, right, over_time, preferred_element_type=jnp.float32)
        full[1] = lax.dot_general(turned, right, over_time, preferred_element_type=jnp.float32)
        vis[0, c] = full[0, pl.ds(first, own), :] * vis_scale
        vis[1, c] = full[1, pl.ds(first, own), :] * vis_scale


def products(volts, weights, own, vis_scale, beam_scale):
    chans, both, tiles = volts.shape
    beams = weights.shape[2]
    block = 8
    return pl.pallas_call(
        functools.partial(product_kernel, own, vis_scale, beam_scale),
        grid=(chans // block,),
        out_shape=(
            jax.ShapeDtypeStruct((2, chans, own, tiles), jnp.float32),
            jax.ShapeDtypeStruct((2, chans, both // 2, beams), jnp.bfloat16),
        ),
        in_specs=[
            pl.BlockSpec((block, both, tiles), lambda i: (i, 0, 0)),
            pl.BlockSpec((block, 2 * tiles, beams), lambda i: (i, 0, 0)),
        ],
        out_specs=(
            pl.BlockSpec((2, block, own, tiles), lambda i: (0, i, 0, 0)),
            pl.BlockSpec((2, block, both // 2, beams), lambda i: (0, i, 0, 0)),
        ),
        scratch_shapes=[pltpu.VMEM((2, tiles, tiles), jnp.float32)],
    )(volts, weights)


def local(voltages, filter_taps, feed_tile, bad_feed, delays):
    channels = filter_taps.shape[1]
    local_frames = voltages.shape[2] // channels
    rim = (TAPS - 1) * channels
    n_dev = lax.axis_size("dev")
    n_sect = lax.axis_size("sect")
    local_chans = channels // n_dev
    total_frames = local_frames * n_dev

    tile_ids = jnp.arange(TILES, dtype=jnp.int32)
    member = (feed_tile[None, :] == tile_ids[:, None]) & (bad_feed[None, :] == 0)
    matrix = jnp.where(member, 1.0, 0.0).astype(jnp.bfloat16)
    partial_value = jnp.einsum(
        "af,zfs->zas", matrix, voltages, preferred_element_type=jnp.float32
    ).astype(jnp.bfloat16)
    summed = lax.psum_scatter(partial_value, "sect", scatter_dimension=1, tiled=True)
    own = summed.shape[1]

    cosine, sine = fourier_tables(channels)
    weights = beam_weights(
        delays, lax.axis_index("dev") * local_chans, local_chans, channels
    )
    summed, cosine, sine, weights = lax.optimization_barrier((summed, cosine, sine, weights))

    history = shifted(summed[:, :, summed.shape[2] - rim :], "dev", 1)
    blocks = pl.pallas_call(
        transform_kernel,
        out_shape=jax.ShapeDtypeStruct((n_dev, 2, local_frames * own, local_chans), jnp.bfloat16),
        in_specs=[VMEM] * 5,
        out_specs=VMEM,
        scratch_shapes=[pltpu.VMEM((2, local_frames * own, channels), jnp.bfloat16)],
    )(summed, history, filter_taps, cosine, sine)
    blocks = blocks.reshape(n_dev, 2 * local_frames * own, local_chans)
    gathered = exchange(blocks, n_sect, n_dev)
    gathered = gathered.reshape(n_sect, n_dev, 2, local_frames, own, local_chans)
    volts = jnp.transpose(gathered, (5, 2, 1, 3, 0, 4)).reshape(
        local_chans, 2 * total_frames, TILES
    )
    vis, beams = products(
        volts, weights, own, 1.0 / (total_frames * FEEDS / TILES), 1.0 / math.sqrt(FEEDS)
    )
    return vis, jnp.transpose(beams, (0, 1, 3, 2))


def solution(mesh):
    return jax.shard_map(
        local,
        mesh=mesh,
        in_specs=(P(None, "sect", "dev"), P(), P("sect"), P("sect"), P("sect", None)),
        out_specs=(P(None, "dev", "sect", None), P(None, "dev", "sect", None)),
        check_vma=False,
    )
```

```python
import functools
import math

import jax
import jax.numpy as jnp
from jax import lax
from jax.experimental import pallas as pl
from jax.experimental.pallas import tpu as pltpu
from jax.sharding import PartitionSpec as P

FEEDS = 2048
TILES = 128
TAPS = 4
LAG = 2
BLOCK = 32


def shifted(x, axis, by):
    size = lax.axis_size(axis)
    pairs = [(i, i + by) for i in range(size) if 0 <= i + by < size]
    return lax.ppermute(x, axis, pairs)


def turn_trig(turns):
    r = turns - jnp.round(turns)
    y = r * math.pi
    q = y * y
    s = 0.0
    for n in (11, 9, 7, 5, 3, 1):
        s = s * q + (-1.0) ** ((n - 1) // 2) / math.factorial(n)
    s = s * y
    c = 0.0
    for n in (12, 10, 8, 6, 4, 2, 0):
        c = c * q + (-1.0) ** (n // 2) / math.factorial(n)
    return 1.0 - 2.0 * s * s, 2.0 * s * c


def fourier_tables(channels):
    low = 32
    c = jnp.arange(channels, dtype=jnp.int32)[None, :]
    k_high = low * jnp.arange(channels // low, dtype=jnp.int32)[:, None]
    k_low = jnp.arange(low, dtype=jnp.int32)[:, None]
    ca, sa = turn_trig((k_high * c % channels).astype(jnp.float32) / channels)
    cb, sb = turn_trig((k_low * c % channels).astype(jnp.float32) / channels)
    factor = 1.0 / math.sqrt(channels)
    ca, sa = (ca * factor)[:, None], (sa * factor)[:, None]
    cb, sb = cb[None], sb[None]
    cosine = (ca * cb - sa * sb).astype(jnp.bfloat16).reshape(channels, channels)
    sine = (sa * cb + ca * sb).astype(jnp.bfloat16).reshape(channels, channels)
    return cosine, sine


def beam_weights(delays, first, count, channels):
    low = 16
    d = delays.T[None]
    high = (first + low * jnp.arange(count // low, dtype=jnp.int32)).astype(jnp.float32)
    ca, sa = turn_trig(d * high[:, None, None] / channels)
    cb, sb = turn_trig(d * jnp.arange(low, dtype=jnp.float32)[:, None, None] / channels)
    ca, sa, cb, sb = ca[:, None], sa[:, None], cb[None], sb[None]
    shape = (count,) + d.shape[1:]
    cosine = (ca * cb - sa * sb).astype(jnp.bfloat16).reshape(shape)
    sine = (sa * cb + ca * sb).astype(jnp.bfloat16).reshape(shape)
    return jnp.concatenate([cosine, sine], axis=1)


VMEM = pl.BlockSpec(memory_space=pltpu.VMEM)


def transform_kernel(summed, history, taps, cosine, sine, out, filtered):
    n_dest, _, _, width = out.shape
    own = summed.shape[1]
    channels = taps.shape[1]
    frames = summed.shape[2] // channels
    for z in range(2):
        for t in range(frames):
            total = 0.0
            for m in range(TAPS):
                if t >= m:
                    block = summed[z, :, (t - m) * channels : (t - m + 1) * channels]
                else:
                    at = t - m + TAPS - 1
                    block = history[z, :, at * channels : (at + 1) * channels]
                total = total + taps[m : m + 1, :] * block.astype(jnp.float32)
            filtered[z, t * own : (t + 1) * own, :] = total.astype(jnp.bfloat16)
    step = max(256, width)
    dot = lambda a, b: jnp.dot(a, b, preferred_element_type=jnp.float32)
    for begin in range(0, channels, step):
        c, s = cosine[:, begin : begin + step], sine[:, begin : begin + step]
        real = (dot(filtered[0], c) + dot(filtered[1], s)).astype(jnp.bfloat16)
        quad = (dot(filtered[1], c) - dot(filtered[0], s)).astype(jnp.bfloat16)
        for j in range(step // width):
            out[begin // width + j, 0] = real[:, j * width : (j + 1) * width]
            out[begin // width + j, 1] = quad[:, j * width : (j + 1) * width]


def exchange_kernel(n_sect, n_dev, src, out, own_sem, a_send, a_recv, x_send, x_recv, y_send, y_recv):
    me_s, me_d = lax.axis_index("sect"), lax.axis_index("dev")
    rows = n_sect // 2
    side, row = lax.rem(me_s, 2), me_s // 2
    across = row * 2 + 1 - side
    others = [(lax.rem(row + j, rows) * 2 + side) for j in range(1, rows)]
    senders = [(lax.rem(row + rows - j, rows) * 2 + side) for j in range(1, rows)]

    barrier = pltpu.get_barrier_semaphore()
    mesh_id = pl.DeviceIdType.MESH
    for o in range(1, n_dev):
        pl.semaphore_signal(barrier, inc=1, device_id=(me_s, lax.rem(me_d + o, n_dev)), device_id_type=mesh_id)
    for s in [across] + others:
        pl.semaphore_signal(barrier, inc=1, device_id=(s, me_d), device_id_type=mesh_id)
    pl.semaphore_wait(barrier, n_dev - 1 + rows)

    def push(source, target, send, recv, device):
        return pltpu.make_async_remote_copy(
            src_ref=source, dst_ref=target, send_sem=send, recv_sem=recv,
            device_id=device, device_id_type=mesh_id,
        )

    order = [0] + [o for pair in zip(range(1, n_dev), range(n_dev - 1, 0, -1)) for o in pair][: n_dev - 1]
    keep = pltpu.make_async_copy(src.at[me_d], out.at[me_s, me_d], own_sem)
    keep.start()
    sends = []
    to_dev = {}
    for o in order[1:]:
        dest = lax.rem(me_d + o, n_dev)
        to_dev[o] = push(src.at[dest], out.at[me_s, me_d], a_send.at[o], a_recv.at[o], (me_s, dest))
        to_dev[o].start()
    keep.wait()

    first = {}

    def spread(o):
        p = lax.rem(me_d + n_dev - o, n_dev)
        here = out.at[me_s, p]
        if o:
            to_dev[o].wait_recv()
        first[o, 0] = push(here, here, x_send.at[o, 0], x_recv.at[o, 0], (across, me_d))
        first[o, 0].start()
        for j in range(1, rows):
            first[o, j] = push(here, here, y_send.at[o, j, 0], y_recv.at[o, j, 0], (others[j - 1], me_d))
            first[o, j].start()

    def relay(o, by_side):
        p = lax.rem(me_d + n_dev - o, n_dev)
        first[o, 0].wait_recv()
        for j in range(1, rows):
            first[o, j].wait_recv()
        for j in range(1, rows):
            if by_side:
                block = out.at[across, p]
                copy = push(block, block, y_send.at[o, j, 1], y_recv.at[o, j, 1], (others[j - 1], me_d))
            else:
                block = out.at[senders[j - 1], p]
                copy = push(block, block, x_send.at[o, j], x_recv.at[o, j], (across, me_d))
            copy.start()
            sends.append(copy)

    lag = LAG
    for i in range(n_dev + lag):
        if i < n_dev:
            spread(order[i])
        if i >= lag:
            relay(order[i - lag], (i - lag) % 2 == 0)
    for copy in sends:
        copy.wait_recv()
    for copy in list(to_dev.values()) + list(first.values()) + sends:
        copy.wait_send()


def exchange(blocks, n_sect, n_dev):
    rows = n_sect // 2
    dma = pltpu.SemaphoreType.DMA
    return pl.pallas_call(
        functools.partial(exchange_kernel, n_sect, n_dev),
        out_shape=jax.ShapeDtypeStruct((n_sect,) + blocks.shape, blocks.dtype),
        in_specs=[VMEM],
        out_specs=VMEM,
        scratch_shapes=[
            dma, dma((n_dev,)), dma((n_dev,)),
            dma((n_dev, rows)), dma((n_dev, rows)),
            dma((n_dev, rows, 2)), dma((n_dev, rows, 2)),
        ],
        compiler_params=pltpu.CompilerParams(
            collective_id=0, has_side_effects=True, vmem_limit_bytes=32 * 2**20
        ),
    )(blocks)


def product_kernel(own, vis_scale, beam_scale, volts, weights, vis, beams, full):
    first = pl.multiple_of(lax.axis_index("sect") * own, own)
    count, both, _ = volts.shape
    half = both // 2

    over_time = (((0,), (0,)), ((), ()))
    for c in range(count):
        real, quad = volts[c, :half, :], volts[c, half:, :]
        straight = jnp.concatenate([real, quad], axis=1)
        turned = jnp.concatenate([quad, -real], axis=1)
        rows = jnp.concatenate([straight, turned], axis=0)
        beam = jnp.dot(rows, weights[c], preferred_element_type=jnp.float32) * beam_scale
        beams[0, c] = beam[:half].astype(jnp.bfloat16)
        beams[1, c] = beam[half:].astype(jnp.bfloat16)
        right = volts[c]
        left = jnp.concatenate([right, jnp.concatenate([quad, -real], axis=0)], axis=1)
        full[c] = lax.dot_general(left, right, over_time, preferred_element_type=jnp.float32)
        tiles = right.shape[1]
        vis[0, c] = full[c, pl.ds(first, own), :] * vis_scale
        vis[1, c] = full[c, pl.ds(pl.multiple_of(first + tiles, own), own), :] * vis_scale


def products(volts, weights, own, vis_scale, beam_scale):
    chans, both, tiles = volts.shape
    beams = weights.shape[2]
    block = BLOCK
    return pl.pallas_call(
        functools.partial(product_kernel, own, vis_scale, beam_scale),
        grid=(chans // block,),
        out_shape=(
            jax.ShapeDtypeStruct((2, chans, own, tiles), jnp.float32),
            jax.ShapeDtypeStruct((2, chans, both // 2, beams), jnp.bfloat16),
        ),
        in_specs=[
            pl.BlockSpec((block, both, tiles), lambda i: (i, 0, 0)),
            pl.BlockSpec((block, 2 * tiles, beams), lambda i: (i, 0, 0)),
        ],
        out_specs=(
            pl.BlockSpec((2, block, own, tiles), lambda i: (0, i, 0, 0)),
            pl.BlockSpec((2, block, both // 2, beams), lambda i: (0, i, 0, 0)),
        ),
        scratch_shapes=[pltpu.VMEM((block, 2 * tiles, tiles), jnp.float32)],
    )(volts, weights)


def local(voltages, filter_taps, feed_tile, bad_feed, delays):
    channels = filter_taps.shape[1]
    local_frames = voltages.shape[2] // channels
    rim = (TAPS - 1) * channels
    n_dev = lax.axis_size("dev")
    n_sect = lax.axis_size("sect")
    local_chans = channels // n_dev
    total_frames = local_frames * n_dev

    tile_ids = jnp.arange(TILES, dtype=jnp.int32)
    member = (feed_tile[None, :] == tile_ids[:, None]) & (bad_feed[None, :] == 0)
    matrix = jnp.where(member, 1.0, 0.0).astype(jnp.bfloat16)
    partial_value = jnp.einsum(
        "af,zfs->zas", matrix, voltages, preferred_element_type=jnp.float32
    ).astype(jnp.bfloat16)
    summed = lax.psum_scatter(partial_value, "sect", scatter_dimension=1, tiled=True)
    own = summed.shape[1]

    cosine, sine = fourier_tables(channels)
    weights = beam_weights(
        delays, lax.axis_index("dev") * local_chans, local_chans, channels
    )
    summed, cosine, sine, weights = lax.optimization_barrier((summed, cosine, sine, weights))

    history = shifted(summed[:, :, summed.shape[2] - rim :], "dev", 1)
    blocks = pl.pallas_call(
        transform_kernel,
        out_shape=jax.ShapeDtypeStruct((n_dev, 2, local_frames * own, local_chans), jnp.bfloat16),
        in_specs=[VMEM] * 5,
        out_specs=VMEM,
        scratch_shapes=[pltpu.VMEM((2, local_frames * own, channels), jnp.bfloat16)],
    )(summed, history, filter_taps, cosine, sine)
    blocks = blocks.reshape(n_dev, 2 * local_frames * own, local_chans)
    gathered = exchange(blocks, n_sect, n_dev)
    gathered = gathered.reshape(n_sect, n_dev, 2, local_frames, own, local_chans)
    volts = jnp.transpose(gathered, (5, 2, 1, 3, 0, 4)).reshape(
        local_chans, 2 * total_frames, TILES
    )
    vis, beams = products(
        volts, weights, own, 1.0 / (total_frames * FEEDS / TILES), 1.0 / math.sqrt(FEEDS)
    )
    return vis, jnp.transpose(beams, (0, 1, 3, 2))


def solution(mesh):
    return jax.shard_map(
        local,
        mesh=mesh,
        in_specs=(P(None, "sect", "dev"), P(), P("sect"), P("sect"), P("sect", None)),
        out_specs=(P(None, "dev", "sect", None), P(None, "dev", "sect", None)),
        check_vma=False,
    )
```

```python
import functools
import math

import jax
import jax.numpy as jnp
from jax import lax
from jax.experimental import pallas as pl
from jax.experimental.pallas import tpu as pltpu
from jax.sharding import PartitionSpec as P

FEEDS = 2048
TILES = 128
TAPS = 4
LAG = 2
BLOCK = 32


def shifted(x, axis, by):
    size = lax.axis_size(axis)
    pairs = [(i, i + by) for i in range(size) if 0 <= i + by < size]
    return lax.ppermute(x, axis, pairs)


def turn_trig(turns):
    r = turns - jnp.round(turns)
    y = r * math.pi
    q = y * y
    s = 0.0
    for n in (11, 9, 7, 5, 3, 1):
        s = s * q + (-1.0) ** ((n - 1) // 2) / math.factorial(n)
    s = s * y
    c = 0.0
    for n in (12, 10, 8, 6, 4, 2, 0):
        c = c * q + (-1.0) ** (n // 2) / math.factorial(n)
    return 1.0 - 2.0 * s * s, 2.0 * s * c


def fourier_tables(channels):
    low = 32
    c = jnp.arange(channels, dtype=jnp.int32)[None, :]
    k_high = low * jnp.arange(channels // low, dtype=jnp.int32)[:, None]
    k_low = jnp.arange(low, dtype=jnp.int32)[:, None]
    ca, sa = turn_trig((k_high * c % channels).astype(jnp.float32) / channels)
    cb, sb = turn_trig((k_low * c % channels).astype(jnp.float32) / channels)
    factor = 1.0 / math.sqrt(channels)
    ca, sa = (ca * factor)[:, None], (sa * factor)[:, None]
    cb, sb = cb[None], sb[None]
    cosine = (ca * cb - sa * sb).astype(jnp.bfloat16).reshape(channels, channels)
    sine = (sa * cb + ca * sb).astype(jnp.bfloat16).reshape(channels, channels)
    return cosine, sine


def beam_weights(delays, first, count, channels):
    low = 16
    d = delays.T[None]
    high = (first + low * jnp.arange(count // low, dtype=jnp.int32)).astype(jnp.float32)
    ca, sa = turn_trig(d * high[:, None, None] / channels)
    cb, sb = turn_trig(d * jnp.arange(low, dtype=jnp.float32)[:, None, None] / channels)
    ca, sa, cb, sb = ca[:, None], sa[:, None], cb[None], sb[None]
    shape = (count,) + d.shape[1:]
    cosine = (ca * cb - sa * sb).astype(jnp.bfloat16).reshape(shape)
    sine = (sa * cb + ca * sb).astype(jnp.bfloat16).reshape(shape)
    return jnp.concatenate([cosine, sine], axis=1)


VMEM = pl.BlockSpec(memory_space=pltpu.VMEM)


def scatter_kernel(n_sect, matrix, volts, out, part, land, b_send, b_recv):
    me_s, me_d = lax.axis_index("sect"), lax.axis_index("dev")
    i, steps = pl.program_id(0), pl.num_programs(0)
    own = matrix.shape[0] // n_sect
    width = volts.shape[2]
    mesh_id = pl.DeviceIdType.MESH

    @pl.when(i == 0)
    def _():
        barrier = pltpu.get_barrier_semaphore()
        for j in range(1, n_sect):
            pl.semaphore_signal(
                barrier, inc=1, device_id=(lax.rem(me_s + j, n_sect), me_d), device_id_type=mesh_id
            )
        pl.semaphore_wait(barrier, n_sect - 1)

    def push(block, j):
        dest = lax.rem(me_s + j, n_sect)
        return pltpu.make_async_remote_copy(
            src_ref=part.at[block, dest], dst_ref=land.at[block, j],
            send_sem=b_send.at[block, j], recv_sem=b_recv.at[block, j],
            device_id=(dest, me_d), device_id_type=mesh_id,
        )

    total = jnp.dot(matrix[...], volts[0], preferred_element_type=jnp.float32)
    total = total.astype(jnp.bfloat16)
    for s in range(n_sect):
        part[i, s] = total[s * own : (s + 1) * own]

    @pl.when(i > 0)
    def _():
        for j in range(1, n_sect):
            push(i - 1, j).start()

    @pl.when(i == steps - 1)
    def _():
        for j in range(1, n_sect):
            push(i, j).start()

        @pl.loop(0, part.shape[0])
        def _(block):
            running = part[block, me_s].astype(jnp.float32)
            for j in range(1, n_sect):
                push(block, j).wait_recv()
                running = running + land[block, j].astype(jnp.float32)
            out[block] = running.astype(jnp.bfloat16)

        @pl.loop(0, part.shape[0])
        def _(block):
            for j in range(1, n_sect):
                push(block, j).wait_send()


def scatter(matrix, voltages, n_sect, width):
    _, feeds, samples = voltages.shape
    across = samples // width
    steps = 2 * across
    own = matrix.shape[0] // n_sect
    dma = pltpu.SemaphoreType.DMA
    return pl.pallas_call(
        functools.partial(scatter_kernel, n_sect),
        grid=(steps,),
        out_shape=jax.ShapeDtypeStruct((steps, own, width), jnp.bfloat16),
        in_specs=[
            pl.BlockSpec(matrix.shape, lambda i: (0, 0)),
            pl.BlockSpec((1, feeds, width), lambda i: (i // across, 0, lax.rem(i, across))),
        ],
        out_specs=VMEM,
        scratch_shapes=[
            pltpu.VMEM((steps, n_sect, own, width), jnp.bfloat16),
            pltpu.VMEM((steps, n_sect, own, width), jnp.bfloat16),
            dma((steps, n_sect)), dma((steps, n_sect)),
        ],
        compiler_params=pltpu.CompilerParams(
            collective_id=1, has_side_effects=True, vmem_limit_bytes=60 * 2**20
        ),
    )(matrix, voltages)


def transform_kernel(summed, history, taps, cosine, sine, out, filtered):
    n_dest, _, _, width = out.shape
    frames, own = summed.shape[1:3]
    channels = taps.shape[1]
    for z in range(2):
        for t in range(frames):
            total = 0.0
            for m in range(TAPS):
                block = summed[z, t - m] if t >= m else history[z, t - m + TAPS - 1]
                total = total + taps[m : m + 1, :] * block.astype(jnp.float32)
            filtered[z, t * own : (t + 1) * own, :] = total.astype(jnp.bfloat16)
    step = max(256, width)
    dot = lambda a, b: jnp.dot(a, b, preferred_element_type=jnp.float32)
    for begin in range(0, channels, step):
        c, s = cosine[:, begin : begin + step], sine[:, begin : begin + step]
        real = (dot(filtered[0], c) + dot(filtered[1], s)).astype(jnp.bfloat16)
        quad = (dot(filtered[1], c) - dot(filtered[0], s)).astype(jnp.bfloat16)
        for j in range(step // width):
            out[begin // width + j, 0] = real[:, j * width : (j + 1) * width]
            out[begin // width + j, 1] = quad[:, j * width : (j + 1) * width]


def exchange_kernel(n_sect, n_dev, src, out, own_sem, a_send, a_recv, x_send, x_recv, y_send, y_recv):
    me_s, me_d = lax.axis_index("sect"), lax.axis_index("dev")
    rows = n_sect // 2
    side, row = lax.rem(me_s, 2), me_s // 2
    across = row * 2 + 1 - side
    others = [(lax.rem(row + j, rows) * 2 + side) for j in range(1, rows)]
    senders = [(lax.rem(row + rows - j, rows) * 2 + side) for j in range(1, rows)]

    barrier = pltpu.get_barrier_semaphore()
    mesh_id = pl.DeviceIdType.MESH
    for o in range(1, n_dev):
        pl.semaphore_signal(barrier, inc=1, device_id=(me_s, lax.rem(me_d + o, n_dev)), device_id_type=mesh_id)
    for s in [across] + others:
        pl.semaphore_signal(barrier, inc=1, device_id=(s, me_d), device_id_type=mesh_id)
    pl.semaphore_wait(barrier, n_dev - 1 + rows)

    def push(source, target, send, recv, device):
        return pltpu.make_async_remote_copy(
            src_ref=source, dst_ref=target, send_sem=send, recv_sem=recv,
            device_id=device, device_id_type=mesh_id,
        )

    order = [0] + [o for pair in zip(range(1, n_dev), range(n_dev - 1, 0, -1)) for o in pair][: n_dev - 1]
    keep = pltpu.make_async_copy(src.at[me_d], out.at[me_s, me_d], own_sem)
    keep.start()
    sends = []
    to_dev = {}
    for o in order[1:]:
        dest = lax.rem(me_d + o, n_dev)
        to_dev[o] = push(src.at[dest], out.at[me_s, me_d], a_send.at[o], a_recv.at[o], (me_s, dest))
        to_dev[o].start()
    keep.wait()

    first = {}

    def spread(o):
        p = lax.rem(me_d + n_dev - o, n_dev)
        here = out.at[me_s, p]
        if o:
            to_dev[o].wait_recv()
        first[o, 0] = push(here, here, x_send.at[o, 0], x_recv.at[o, 0], (across, me_d))
        first[o, 0].start()
        for j in range(1, rows):
            first[o, j] = push(here, here, y_send.at[o, j, 0], y_recv.at[o, j, 0], (others[j - 1], me_d))
            first[o, j].start()

    def relay(o, by_side):
        p = lax.rem(me_d + n_dev - o, n_dev)
        first[o, 0].wait_recv()
        for j in range(1, rows):
            first[o, j].wait_recv()
        for j in range(1, rows):
            if by_side:
                block = out.at[across, p]
                copy = push(block, block, y_send.at[o, j, 1], y_recv.at[o, j, 1], (others[j - 1], me_d))
            else:
                block = out.at[senders[j - 1], p]
                copy = push(block, block, x_send.at[o, j], x_recv.at[o, j], (across, me_d))
            copy.start()
            sends.append(copy)

    lag = LAG
    for i in range(n_dev + lag):
        if i < n_dev:
            spread(order[i])
        if i >= lag:
            relay(order[i - lag], (i - lag) % 2 == 0)
    for copy in sends:
        copy.wait_recv()
    for copy in list(to_dev.values()) + list(first.values()) + sends:
        copy.wait_send()


def exchange(blocks, n_sect, n_dev):
    rows = n_sect // 2
    dma = pltpu.SemaphoreType.DMA
    return pl.pallas_call(
        functools.partial(exchange_kernel, n_sect, n_dev),
        out_shape=jax.ShapeDtypeStruct((n_sect,) + blocks.shape, blocks.dtype),
        in_specs=[VMEM],
        out_specs=VMEM,
        scratch_shapes=[
            dma, dma((n_dev,)), dma((n_dev,)),
            dma((n_dev, rows)), dma((n_dev, rows)),
            dma((n_dev, rows, 2)), dma((n_dev, rows, 2)),
        ],
        compiler_params=pltpu.CompilerParams(
            collective_id=0, has_side_effects=True, vmem_limit_bytes=32 * 2**20
        ),
    )(blocks)


def product_kernel(own, vis_scale, beam_scale, volts, weights, vis, beams, full):
    first = pl.multiple_of(lax.axis_index("sect") * own, own)
    count, both, _ = volts.shape
    half = both // 2

    over_time = (((0,), (0,)), ((), ()))
    for c in range(count):
        real, quad = volts[c, :half, :], volts[c, half:, :]
        straight = jnp.concatenate([real, quad], axis=1)
        turned = jnp.concatenate([quad, -real], axis=1)
        rows = jnp.concatenate([straight, turned], axis=0)
        beam = jnp.dot(rows, weights[c], preferred_element_type=jnp.float32) * beam_scale
        beams[0, c] = beam[:half].astype(jnp.bfloat16)
        beams[1, c] = beam[half:].astype(jnp.bfloat16)
        right = volts[c]
        left = jnp.concatenate([right, jnp.concatenate([quad, -real], axis=0)], axis=1)
        full[c] = lax.dot_general(left, right, over_time, preferred_element_type=jnp.float32)
        tiles = right.shape[1]
        vis[0, c] = full[c, pl.ds(first, own), :] * vis_scale
        vis[1, c] = full[c, pl.ds(pl.multiple_of(first + tiles, own), own), :] * vis_scale


def products(volts, weights, own, vis_scale, beam_scale):
    chans, both, tiles = volts.shape
    beams = weights.shape[2]
    block = BLOCK
    return pl.pallas_call(
        functools.partial(product_kernel, own, vis_scale, beam_scale),
        grid=(chans // block,),
        out_shape=(
            jax.ShapeDtypeStruct((2, chans, own, tiles), jnp.float32),
            jax.ShapeDtypeStruct((2, chans, both // 2, beams), jnp.bfloat16),
        ),
        in_specs=[
            pl.BlockSpec((block, both, tiles), lambda i: (i, 0, 0)),
            pl.BlockSpec((block, 2 * tiles, beams), lambda i: (i, 0, 0)),
        ],
        out_specs=(
            pl.BlockSpec((2, block, own, tiles), lambda i: (0, i, 0, 0)),
            pl.BlockSpec((2, block, both // 2, beams), lambda i: (0, i, 0, 0)),
        ),
        scratch_shapes=[pltpu.VMEM((block, 2 * tiles, tiles), jnp.float32)],
    )(volts, weights)


def local(voltages, filter_taps, feed_tile, bad_feed, delays):
    channels = filter_taps.shape[1]
    local_frames = voltages.shape[2] // channels
    n_dev = lax.axis_size("dev")
    n_sect = lax.axis_size("sect")
    local_chans = channels // n_dev
    total_frames = local_frames * n_dev

    tile_ids = jnp.arange(TILES, dtype=jnp.int32)
    member = (feed_tile[None, :] == tile_ids[:, None]) & (bad_feed[None, :] == 0)
    matrix = jnp.where(member, 1.0, 0.0).astype(jnp.bfloat16)
    cosine, sine = fourier_tables(channels)
    weights = beam_weights(
        delays, lax.axis_index("dev") * local_chans, local_chans, channels
    )
    own = TILES // n_sect
    summed = scatter(matrix, voltages, n_sect, channels).reshape(2, local_frames, own, channels)

    history = shifted(summed[:, local_frames - (TAPS - 1) :], "dev", 1)
    blocks = pl.pallas_call(
        transform_kernel,
        out_shape=jax.ShapeDtypeStruct((n_dev, 2, local_frames * own, local_chans), jnp.bfloat16),
        in_specs=[VMEM] * 5,
        out_specs=VMEM,
        scratch_shapes=[pltpu.VMEM((2, local_frames * own, channels), jnp.bfloat16)],
    )(summed, history, filter_taps, cosine, sine)
    blocks = blocks.reshape(n_dev, 2 * local_frames * own, local_chans)
    gathered = exchange(blocks, n_sect, n_dev)
    gathered = gathered.reshape(n_sect, n_dev, 2, local_frames, own, local_chans)
    volts = jnp.transpose(gathered, (5, 2, 1, 3, 0, 4)).reshape(
        local_chans, 2 * total_frames, TILES
    )
    vis, beams = products(
        volts, weights, own, 1.0 / (total_frames * FEEDS / TILES), 1.0 / math.sqrt(FEEDS)
    )
    return vis, jnp.transpose(beams, (0, 1, 3, 2))


def solution(mesh):
    return jax.shard_map(
        local,
        mesh=mesh,
        in_specs=(P(None, "sect", "dev"), P(), P("sect"), P("sect"), P("sect", None)),
        out_specs=(P(None, "dev", "sect", None), P(None, "dev", "sect", None)),
        check_vma=False,
    )
```
